32 devices in a mesh: group: 4 (over y, x), member: 8 (over z, core).
Axes of the slice: x: 2, y: 2, z: 4, core: 2. Of those that a mesh axis runs over, the one named last changes fastest.
Arguments:
- activations: bfloat16 [4, 1024, 2048], P('group', 'member'), may hold values from -6 to 6
- lengths: int32 [4, 8], P('group'), may hold values from 1 to 128, 576 in all within a row
- assignment: int32 [4, 8], P('group'), may hold values from 0 to 7, each once within a row
- owners: int32 [4], replicated, may hold values from 0 to 3
- prefix_cache: bfloat16 [4, 8192, 256], P('group', 'member'), may hold values from -244 to 244
- first_gain: float32 [2048], replicated, may hold values from 0.1 to 1.9
- first_bias: float32 [2048], replicated, may hold values from -3 to 3
- query_weight: bfloat16 [2048, 2048], replicated, may hold values from -0.125 to 0.125
- keyval_weight: bfloat16 [2048, 256], replicated, may hold values from -0.4375 to 0.4375
- output_weight: bfloat16 [2048, 2048], replicated, may hold values from -0.125 to 0.125
- second_gain: float32 [2048], replicated, may hold values from 0.1 to 1.9
- second_bias: float32 [2048], replicated, may hold values from -3 to 3
- expand_weight: bfloat16 [2048, 8192], P(None, 'member'), may hold values from -0.125 to 0.125
- contract_weight: bfloat16 [8192, 2048], P('member'), may hold values from -0.0625 to 0.0625
Outputs:
- layer_output: bfloat16 [4, 1024, 2048], P('group', 'member')
The draws below stay inside these ranges and needn't reach their ends.
Inputs may be any that keep to these rules, and one draw needn't show every extreme that they name: Each row of lengths sums to 576 and its longest entry is 128. Each row of assignment names every request of its group once. `owners`: several groups may attend the same cache slot.
All inputs are finite; a program needn't handle non-finite values.
Results may differ from the reference program's by a relative error of at most 0.011.
The reference program's roundings to bfloat16 on the way count: a program that leaves them out, or rounds other values in their place, can miss the bound.
Values may be sent and summed in bfloat16 or wider, within the bound.
No kernel may reach another device: no remote copies, remote signals or barrier semaphores. Data moves between devices by JAX's collectives and lax.ppermute only.
A program may use at most 128 MiB of HBM per device.

```python
import math
import jax
import jax.numpy as jnp
import numpy as np
from jax import lax

D = 2048
H = 16
FF = 8192
HD = 128
TOK_DEV = 128
GROUPS = 4
MEMBERS = 8
PLEN = 8192
SLOTS = 1024
TOTAL_ROW = 576
FF_DEV = 1024


def draw_prefix_cache(key, part):
    streams = jax.random.split(key, 1)
    shape = (GROUPS, PLEN, 2 * HD)
    base = jnp.clip(jax.random.normal(streams[0], shape, jnp.float32), -5.0, 5.0)
    column = lax.broadcasted_iota(jnp.int32, shape, 2)
    scaled = jnp.where(column < HD, 2.5 * base, base)
    return scaled.astype(jnp.bfloat16)


def set_ends(drawn, key, low, largest):
    index_at = [jax.random.randint(jax.random.fold_in(key, axis), (), 0, length) for axis, length in enumerate(drawn.shape)]
    widest = drawn.shape.index(max(drawn.shape))
    beside = index_at[:widest] + [(index_at[widest] + 1) % drawn.shape[widest]] + index_at[widest + 1:]
    return drawn.at[tuple(index_at)].set(low).at[tuple(beside)].set(largest)


def shard_levels(rng, extent, shards, smallest, largest):
    level, own = 1.0, jax.random.fold_in(rng, 6)
    for axis_at, shards_of in shards:
        heights = jnp.exp(jax.random.uniform(jax.random.fold_in(own, axis_at), (shards_of,), jnp.float32, smallest / len(shards), largest / len(shards)))
        level = level * jnp.repeat(heights, extent[axis_at] // shards_of).reshape([-1 if axis == axis_at else 1 for axis in range(len(extent))])
    return level


def split_up(number_of, total, bound, skew):
    portions = [(1 << 20) // math.isqrt(grade ** skew) + 1 for grade in range(2, number_of + 1)]
    spare, holding = total - bound - (number_of - 1), [1] * (number_of - 1)
    while spare > 0:
        movable = [i for i in range(number_of - 1) if holding[i] < bound]
        pool, left = sum([portions[i] for i in movable]), spare
        for i in movable:
            addition = min(bound - holding[i], max(1, left * portions[i] // pool), spare)
            holding[i] = holding[i] + addition
            spare = spare - addition
    return np.array([bound] + holding)


def ragged(stream_key, amount, total, limit, skew):
    if amount == 2:
        one = jax.random.randint(stream_key, (), max(1, total - limit), min(limit, total - 1) + 1)
        return jnp.stack([one, total - one])
    tallies = jnp.asarray(split_up(amount, total, limit, skew), jnp.int32)
    twos = (amount - 1) // 2
    donor, sink = tallies[1:1 + 2 * twos:2], tallies[2:2 + 2 * twos:2]
    margin = jnp.minimum(donor - 1, limit - sink)
    passed = jax.random.randint(jax.random.fold_in(stream_key, 1), (twos,), 0, 1 << 20) % (margin + 1)
    tallies = tallies.at[1:1 + 2 * twos:2].set(donor - passed).at[2:2 + 2 * twos:2].set(sink + passed)
    return tallies[jax.random.permutation(jax.random.fold_in(stream_key, 2), amount)]


def noise(own_key, dims, scale, most, cuts=(), kind=jnp.bfloat16):
    drawn = jax.random.normal(own_key, dims, jnp.float32) * scale
    if len(cuts) > 0:
        drawn = shard_levels(own_key, dims, cuts, -0.22, 0.18) * drawn
    return jnp.clip(drawn, min=-most, max=most).astype(kind)


def setup_inputs(seed: int = 0) -> dict:
    splits = jax.random.split(jax.random.key(seed), 15)
    activations = noise(splits[0], (GROUPS, SLOTS, D), 1.0, 6.0, ((0, 4), (1, 8)))
    lengths = jax.vmap(lambda own: ragged(own, MEMBERS, TOTAL_ROW, TOK_DEV, 2))(jax.random.split(splits[1], GROUPS)).reshape((GROUPS, MEMBERS)).astype(jnp.int32)
    assignment = jax.vmap(lambda own: jax.random.permutation(own, MEMBERS))(jax.random.split(splits[2], GROUPS)).reshape((GROUPS, MEMBERS)).astype(jnp.int32)
    owners = set_ends(jax.random.randint(splits[3], (GROUPS,), 0, GROUPS), jax.random.fold_in(splits[3], 1), 0, GROUPS - 1).astype(jnp.int32)
    prefix_cache = draw_prefix_cache(jax.random.fold_in(splits[14], 71), 0)
    first_gain = jnp.clip(1.0 + 0.18 * jax.random.normal(splits[5], (D,), jnp.float32), 0.1, 1.9)
    first_bias = noise(splits[6], (D,), 0.3, 3.0, (), jnp.float32)
    query_weight = noise(splits[7], (D, D), D ** -0.5, 0.125)
    keyval_weight = noise(splits[8], (D, 2 * HD), (D // 12) ** -0.5, 0.4375)
    output_weight = noise(splits[9], (D, D), D ** -0.5, 0.125)
    second_gain = jnp.clip(1.0 + 0.18 * jax.random.normal(splits[10], (D,), jnp.float32), 0.1, 1.9)
    second_bias = noise(splits[11], (D,), 0.3, 3.0, (), jnp.float32)
    expand_weight = noise(splits[12], (D, FF), D ** -0.5, 0.125, ((1, 8),))
    contract_weight = noise(splits[13], (FF, D), FF ** -0.5, 0.0625, ((0, 8),))
    return dict(activations=activations, lengths=lengths, assignment=assignment, owners=owners, prefix_cache=prefix_cache, first_gain=first_gain, first_bias=first_bias, query_weight=query_weight, keyval_weight=keyval_weight, output_weight=output_weight, second_gain=second_gain, second_bias=second_bias, expand_weight=expand_weight, contract_weight=contract_weight)


EPSILON = 1e-05
NEGATIVE = -1e+30

def layer_norm(values, gain, bias):
    average = lax.optimization_barrier(jnp.mean(values, axis=-1, keepdims=True))
    centered = values - average
    spread = lax.optimization_barrier(jnp.mean(centered * centered, axis=-1, keepdims=True))
    return centered * lax.rsqrt(spread + EPSILON) * gain + bias

def rounded(values):
    return lax.optimization_barrier(values.astype(jnp.bfloat16)).astype(jnp.float32)

def slot_attention(queries, keys_values, prefix):
    scaling = 1.0 / HD ** 0.5
    query_wide = queries.astype(jnp.float32)
    prefix_keys = prefix[:, :HD].astype(jnp.float32)
    prefix_values = prefix[:, HD:].astype(jnp.float32)
    own_keys = keys_values[:, :HD].astype(jnp.float32)
    own_values = keys_values[:, HD:].astype(jnp.float32)
    prefix_scores = jnp.einsum('thd,pd->thp', query_wide, prefix_keys, precision=lax.Precision.HIGHEST) * scaling
    own_scores = jnp.einsum('thd,sd->ths', query_wide, own_keys, precision=lax.Precision.HIGHEST) * scaling
    positions = jnp.arange(TOK_DEV, dtype=jnp.int32)
    causal = positions[None, :] <= positions[:, None]
    own_scores = jnp.where(causal[:, None, :], own_scores, NEGATIVE)
    highest = jnp.maximum(lax.optimization_barrier(jnp.max(prefix_scores, axis=-1, keepdims=True)), lax.optimization_barrier(jnp.max(own_scores, axis=-1, keepdims=True)))
    prefix_exp = jnp.exp(prefix_scores - highest)
    own_exp = jnp.exp(own_scores - highest)
    denominator = lax.optimization_barrier(jnp.sum(prefix_exp, axis=-1)) + lax.optimization_barrier(jnp.sum(own_exp, axis=-1))
    weighted = jnp.einsum('thp,pd->thd', rounded(prefix_exp), prefix_values, precision=lax.Precision.HIGHEST)
    weighted = weighted + jnp.einsum('ths,sd->thd', rounded(own_exp), own_values, precision=lax.Precision.HIGHEST)
    return (weighted / denominator[..., None]).astype(jnp.bfloat16).reshape(TOK_DEV, H * HD)

def reference(activations, lengths, assignment, owners, prefix_cache, first_gain, first_bias, query_weight, keyval_weight, output_weight, second_gain, second_bias, expand_weight, contract_weight):

    def one_group(inputs):
        tokens, length_row, assign_row, owner_row = inputs
        prefix = lax.dynamic_index_in_dim(prefix_cache, owner_row, 0, keepdims=False)
        tokens_wide = tokens.astype(jnp.float32)
        normed = layer_norm(tokens_wide, first_gain, first_bias).astype(jnp.bfloat16)
        queries = jnp.dot(normed, query_weight, preferred_element_type=jnp.float32).astype(jnp.bfloat16)
        keys_values = jnp.dot(normed, keyval_weight, preferred_element_type=jnp.float32).astype(jnp.bfloat16)

        def attend_slot(operands):
            return slot_attention(operands[0], operands[1], prefix)
        attended = lax.map(attend_slot, (queries.reshape(MEMBERS, TOK_DEV, H, HD), keys_values.reshape(MEMBERS, TOK_DEV, 2 * HD)))
        attended = attended.reshape(SLOTS, H * HD)
        residual = tokens_wide + jnp.dot(attended, output_weight, preferred_element_type=jnp.float32)
        second = layer_norm(residual, second_gain, second_bias).astype(jnp.bfloat16)
        hidden = jax.nn.gelu(jnp.dot(second, expand_weight, preferred_element_type=jnp.float32), approximate=True).astype(jnp.bfloat16)
        hidden_parts = hidden.reshape(SLOTS, MEMBERS, FF_DEV).transpose(1, 0, 2)
        weight_parts = contract_weight.reshape(MEMBERS, FF_DEV, D)

        def add_part(running, operands):
            partial_value = jnp.dot(operands[0], operands[1], preferred_element_type=jnp.float32)
            return (running + rounded(partial_value), None)
        summed, _ = lax.scan(add_part, jnp.zeros((SLOTS, D), jnp.float32), (hidden_parts, weight_parts))
        request_lengths = jnp.take(length_row, assign_row)
        positions = jnp.arange(TOK_DEV, dtype=jnp.int32)
        is_live = (positions[None, :] < request_lengths[:, None]).reshape(SLOTS, 1)
        return jnp.where(is_live, residual + summed, 0.0).astype(jnp.bfloat16)
    return lax.map(one_group, (activations, lengths, assignment, owners))
```

```python
import functools
import math

import jax
import jax.numpy as jnp
from jax import lax
from jax.experimental import pallas as pl
from jax.experimental.pallas import tpu as pltpu
from jax.sharding import PartitionSpec as P

EPSILON = 1e-05
NEGATIVE = -1e30
HEADS_AT_ONCE = 2


def layer_norm(values, gain, bias):
    average = jnp.mean(values, axis=-1, keepdims=True)
    centered = values - average
    spread = jnp.mean(centered * centered, axis=-1, keepdims=True)
    return centered * lax.rsqrt(spread + EPSILON) * gain + bias


def pick_value(table, wanted):
    slots_at = lax.broadcasted_iota(jnp.int32, table.shape, 0)
    return jnp.sum(jnp.where(slots_at == wanted, table, 0))


def ring_order(chips):
    return list(range(0, 1)) + list(range(1, chips, 2)) + list(range(chips - 2 + chips % 2, 0, -2))


def attend_kernel(first, last, head_size, *refs):
    refs = list(refs)
    query_ref = refs.pop(0)
    if first:
        own_ref = refs.pop(0)
    else:
        weighted_in, highest_in, denominator_in = refs[:3]
        del refs[:3]
    outs = 1 if last else 3
    block_refs, out_refs = refs[:-outs], refs[-outs:]
    rows = query_ref.shape[0]
    factor = math.log2(math.e) / math.sqrt(head_size)
    queries = jnp.concatenate(
        [query_ref[:, h * head_size : (h + 1) * head_size] for h in range(HEADS_AT_ONCE)], axis=0
    )

    def raw_scores(keys):
        return lax.dot_general(
            queries, keys, (((1,), (1,)), ((), ())), preferred_element_type=jnp.float32
        )

    def apply(scores, values, highest):
        exponent = jnp.exp2((scores - highest) * factor)
        total = jnp.sum(exponent, axis=-1, keepdims=True)
        product = jnp.dot(exponent.astype(jnp.bfloat16), values, preferred_element_type=jnp.float32)
        return product, total

    if first:
        scores = raw_scores(own_ref[:, :head_size])
        row_at = lax.broadcasted_iota(jnp.int32, scores.shape, 0) % rows
        column_at = lax.broadcasted_iota(jnp.int32, scores.shape, 1)
        scores = jnp.where(column_at <= row_at, scores, NEGATIVE)
        highest = jnp.max(scores, axis=-1, keepdims=True)
        weighted, denominator = apply(scores, own_ref[:, head_size:], highest)
    else:
        weighted = jnp.concatenate(
            [weighted_in[:, h * head_size : (h + 1) * head_size] for h in range(HEADS_AT_ONCE)], axis=0
        )
        highest = jnp.concatenate([highest_in[h] for h in range(HEADS_AT_ONCE)], axis=0)
        denominator = jnp.concatenate([denominator_in[h] for h in range(HEADS_AT_ONCE)], axis=0)
    for block_ref in block_refs:
        extent = block_ref.shape[0]
        stride = math.gcd(extent, 1024)
        for start in range(0, extent, stride):
            scores = raw_scores(block_ref[start : start + stride, :head_size])
            highest_next = jnp.maximum(highest, jnp.max(scores, axis=-1, keepdims=True))
            rescale = jnp.exp2((highest - highest_next) * factor)
            product, total = apply(scores, block_ref[start : start + stride, head_size:], highest_next)
            weighted = weighted * rescale + product
            denominator = denominator * rescale + total
            highest = highest_next
    if last:
        weighted = weighted / denominator
    for h in range(HEADS_AT_ONCE):
        part = weighted[h * rows : (h + 1) * rows]
        out_refs[0][:, h * head_size : (h + 1) * head_size] = part.astype(out_refs[0].dtype)
        if not last:
            out_refs[1][h] = highest[h * rows : (h + 1) * rows]
            out_refs[2][h] = denominator[h * rows : (h + 1) * rows]


def attend(queries, own, state, blocks, last, head_size):
    rows, width = queries.shape
    heads = width // head_size
    wide = HEADS_AT_ONCE * head_size
    first = state is None
    flat = pl.BlockSpec((rows, wide), lambda i: (0, i))
    stat = pl.BlockSpec((HEADS_AT_ONCE, rows, 1), lambda i: (i, 0, 0))
    whole = lambda array: pl.BlockSpec(array.shape, lambda i: (0, 0))
    in_specs = [flat] + ([whole(own)] if first else [flat, stat, stat]) + [whole(b) for b in blocks]
    operands = [queries] + ([own] if first else list(state)) + list(blocks)
    if last:
        out_specs = flat
        out_shape = jax.ShapeDtypeStruct((rows, width), jnp.bfloat16)
    else:
        out_specs = [flat, stat, stat]
        out_shape = [jax.ShapeDtypeStruct((rows, width), jnp.float32)] + [
            jax.ShapeDtypeStruct((heads, rows, 1), jnp.float32)
        ] * 2
    keys = sum(b.shape[0] for b in blocks) + (own.shape[0] if first else 0)
    return pl.pallas_call(
        functools.partial(attend_kernel, first, last, head_size),
        grid=(heads // HEADS_AT_ONCE,),
        in_specs=in_specs,
        out_specs=out_specs,
        out_shape=out_shape,
        cost_estimate=pl.CostEstimate(
            flops=4 * rows * width * keys,
            bytes_accessed=2 * keys * 2 * head_size + 8 * rows * width,
            transcendentals=rows * heads * keys,
        ),
        compiler_params=pltpu.CompilerParams(vmem_limit_bytes=32 * 1024 * 1024),
    )(*operands)


def choose_prefix(own, owners, sizes):
    groups, members = sizes
    group_index = lax.axis_index("group")
    member_index = lax.axis_index("member")
    wanted = pick_value(owners, group_index)
    if groups != 4:
        every_block = lax.all_gather(own, "group", axis=0)
        return lax.dynamic_index_in_dim(every_block, wanted, 0, keepdims=False)
    near = 1 + member_index % 2
    far = 3 - near

    def step(block, flip):
        pairs = [
            (g * members + m, (g ^ (flip ^ (3 * (m % 2)))) * members + m)
            for g in range(groups)
            for m in range(members)
        ]
        return lax.ppermute(block, ("group", "member"), pairs)

    beside = step(own, 1)
    wanted_there = pick_value(owners, group_index ^ far)
    passed = jnp.where(wanted_there == (group_index ^ near), beside, own)
    across = step(passed, 2)
    return jnp.where(
        wanted == group_index, own, jnp.where(wanted == (group_index ^ near), beside, across)
    )


def shards(
    sizes,
    activations,
    lengths,
    assignment,
    owners,
    prefix_cache,
    first_gain,
    first_bias,
    query_weight,
    keyval_weight,
    output_weight,
    second_gain,
    second_bias,
    expand_weight,
    contract_weight,
):
    groups, members = sizes
    chips = members // 2
    order = ring_order(chips)
    after = {order[i]: order[(i + 1) % chips] for i in range(chips)}
    ring_pairs = [(2 * z + c, 2 * after[z] + c) for z in range(chips) for c in range(2)]
    swap_pairs = [(m, m ^ 1) for m in range(members)]
    ring = lambda block: lax.ppermute(block, "member", ring_pairs)
    swap = lambda block: lax.ppermute(block, "member", swap_pairs)

    member_index = lax.axis_index("member")
    request = pick_value(assignment[0], member_index)
    length_here = pick_value(lengths[0], request)
    tokens = activations[0]
    row_count = tokens.shape[0]
    head_size = prefix_cache.shape[2] // 2

    block = choose_prefix(prefix_cache[0], owners, sizes)
    expand_other = swap(expand_weight)
    contract_other = swap(contract_weight)

    tokens_wide = tokens.astype(jnp.float32)
    normed = layer_norm(tokens_wide, first_gain, first_bias).astype(jnp.bfloat16)
    queries = jnp.dot(normed, query_weight, preferred_element_type=jnp.float32).astype(jnp.bfloat16)
    keys_values = jnp.dot(normed, keyval_weight, preferred_element_type=jnp.float32).astype(
        jnp.bfloat16
    )

    state = None
    for step in range(chips):
        later = ring(block) if step < chips - 1 else None
        other = swap(block)
        state = attend(queries, keys_values, state, [block, other], step == chips - 1, head_size)
        block = later
    attended = state

    residual = tokens_wide + jnp.dot(attended, output_weight, preferred_element_type=jnp.float32)
    second = layer_norm(residual, second_gain, second_bias).astype(jnp.bfloat16)

    def feed_forward(rows):
        total = None
        for expand, contract in ((expand_weight, contract_weight), (expand_other, contract_other)):
            hidden = jax.nn.gelu(
                jnp.dot(rows, expand, preferred_element_type=jnp.float32), approximate=True
            ).astype(jnp.bfloat16)
            part = jnp.dot(hidden, contract, preferred_element_type=jnp.float32)
            total = part if total is None else total + part
        return total

    rows, summed = second, None
    for step in range(1, chips):
        rows = ring(rows)
        part = feed_forward(rows)
        part = part if summed is None else part + summed.astype(jnp.float32)
        summed = ring(part.astype(jnp.bfloat16))
    total = residual + feed_forward(second) + summed.astype(jnp.float32)
    is_live = lax.broadcasted_iota(jnp.int32, (row_count, 1), 0) < length_here
    return jnp.where(is_live, total, 0.0).astype(jnp.bfloat16)[None]


def solution(mesh):
    sizes = (mesh.shape["group"], mesh.shape["member"])
    return jax.shard_map(
        functools.partial(shards, sizes),
        mesh=mesh,
        in_specs=(
            P("group", "member", None),
            P("group", None),
            P("group", None),
            P(),
            P("group", "member", None),
            P(),
            P(),
            P(),
            P(),
            P(),
            P(),
            P(),
            P(None, "member"),
            P("member", None),
        ),
        out_specs=P("group", "member", None),
        check_vma=False,
    )
```

```python
import functools
import math

import jax
import jax.numpy as jnp
from jax import lax
from jax.experimental import pallas as pl
from jax.experimental.pallas import tpu as pltpu
from jax.sharding import PartitionSpec as P

EPSILON = 1e-05
NEGATIVE = -1e30
HEADS_AT_ONCE = 8
HEADS_STACKED = 2


def layer_norm(values, gain, bias):
    average = jnp.mean(values, axis=-1, keepdims=True)
    centered = values - average
    spread = jnp.mean(centered * centered, axis=-1, keepdims=True)
    return centered * lax.rsqrt(spread + EPSILON) * gain + bias


def pick_value(table, wanted):
    slots_at = lax.broadcasted_iota(jnp.int32, table.shape, 0)
    return jnp.sum(jnp.where(slots_at == wanted, table, 0))


def ring_order(chips):
    return list(range(0, 1)) + list(range(1, chips, 2)) + list(range(chips - 2 + chips % 2, 0, -2))


def attend_kernel(first, last, head_size, group, *refs):
    refs = list(refs)
    query_ref = refs.pop(0)
    if first:
        own_ref = refs.pop(0)
    else:
        weighted_in, highest_in, denominator_in = refs[:3]
        del refs[:3]
    outs = 1 if last else 3
    block_refs, out_refs = refs[:-outs], refs[-outs:]
    rows = query_ref.shape[0]
    heads = query_ref.shape[1] // head_size

    def stacked(ref, start):
        return jnp.concatenate(
            [ref[:, (start + h) * head_size : (start + h + 1) * head_size] for h in range(group)], axis=0
        )

    def all_scores(start):
        queries = stacked(query_ref, start)
        result = []
        for ref in ([own_ref] if first else []) + block_refs:
            scores = lax.dot_general(
                queries, ref[:, :head_size], (((1,), (1,)), ((), ())), preferred_element_type=jnp.float32
            )
            result.append(scores)
        if first:
            row_at = lax.broadcasted_iota(jnp.int32, result[0].shape, 0) % rows
            column_at = lax.broadcasted_iota(jnp.int32, result[0].shape, 1)
            result[0] = jnp.where(column_at <= row_at, result[0], NEGATIVE)
        return result

    def fold(start, scores):
        highest = None
        for part in scores:
            top = jnp.max(part, axis=-1, keepdims=True)
            highest = top if highest is None else jnp.maximum(highest, top)
        weighted, denominator = None, None
        if not first:
            before = jnp.concatenate([highest_in[start + h] for h in range(group)], axis=0)
            highest = jnp.maximum(highest, before)
            rescale = jnp.exp2(before - highest)
            weighted = stacked(weighted_in, start) * rescale
            denominator = (
                jnp.concatenate([denominator_in[start + h] for h in range(group)], axis=0) * rescale
            )
        for part, ref in zip(scores, ([own_ref] if first else []) + block_refs):
            exponent = jnp.exp2(part - highest)
            total = jnp.sum(exponent, axis=-1, keepdims=True)
            product = jnp.dot(
                exponent.astype(jnp.bfloat16), ref[:, head_size:], preferred_element_type=jnp.float32
            )
            weighted = product if weighted is None else weighted + product
            denominator = total if denominator is None else denominator + total
        if last:
            weighted = weighted / denominator
        for h in range(group):
            at = start + h
            part = slice(h * rows, (h + 1) * rows)
            out_refs[0][:, at * head_size : (at + 1) * head_size] = weighted[part].astype(out_refs[0].dtype)
            if not last:
                out_refs[1][at] = highest[part]
                out_refs[2][at] = denominator[part]

    scores = all_scores(0)
    for start in range(0, heads, group):
        following = all_scores(start + group) if start + group < heads else None
        fold(start, scores)
        scores = following


def attend(queries, own, state, blocks, last, head_size):
    rows, width = queries.shape
    heads = width // head_size
    at_once = math.gcd(heads, HEADS_AT_ONCE)
    wide = at_once * head_size
    first = state is None
    flat = pl.BlockSpec((rows, wide), lambda i: (0, i))
    stat = pl.BlockSpec((at_once, rows, 1), lambda i: (i, 0, 0))
    whole = lambda array: pl.BlockSpec(array.shape, lambda i: (0, 0))
    in_specs = [flat] + ([whole(own)] if first else [flat, stat, stat]) + [whole(b) for b in blocks]
    operands = [queries] + ([own] if first else list(state)) + list(blocks)
    if last:
        out_specs = flat
        out_shape = jax.ShapeDtypeStruct((rows, width), jnp.bfloat16)
    else:
        out_specs = [flat, stat, stat]
        out_shape = [jax.ShapeDtypeStruct((rows, width), jnp.float32)] + [
            jax.ShapeDtypeStruct((heads, rows, 1), jnp.float32)
        ] * 2
    keys = sum(b.shape[0] for b in blocks) + (own.shape[0] if first else 0)
    return pl.pallas_call(
        functools.partial(attend_kernel, first, last, head_size, math.gcd(at_once, HEADS_STACKED)),
        grid=(heads // at_once,),
        in_specs=in_specs,
        out_specs=out_specs,
        out_shape=out_shape,
        cost_estimate=pl.CostEstimate(
            flops=4 * rows * width * keys,
            bytes_accessed=2 * keys * 2 * head_size + 8 * rows * width,
            transcendentals=rows * heads * keys,
        ),
        compiler_params=pltpu.CompilerParams(vmem_limit_bytes=24 * 1024 * 1024),
    )(*operands)


def hold_kernel(count, *refs):
    sources, held, semaphores = refs[:count], refs[count:-1], refs[-1]
    copies = [
        pltpu.make_async_copy(sources[i], held[i], semaphores.at[i]) for i in range(count)
    ]
    for copy in copies:
        copy.start()
    for copy in copies:
        copy.wait()


def hold(*weights):
    count = len(weights)
    size = sum(w.size * w.dtype.itemsize for w in weights)
    return pl.pallas_call(
        functools.partial(hold_kernel, count),
        in_specs=[pl.BlockSpec(memory_space=pl.ANY)] * count,
        out_specs=[pl.BlockSpec(memory_space=pltpu.VMEM)] * count,
        out_shape=[pltpu.VMEM(w.shape, w.dtype) for w in weights],
        scratch_shapes=[pltpu.SemaphoreType.DMA((count,))],
        cost_estimate=pl.CostEstimate(flops=0, bytes_accessed=size, transcendentals=0),
        compiler_params=pltpu.CompilerParams(vmem_limit_bytes=4 * 1024 * 1024),
    )(*weights)


def feed_forward_kernel(count, rows_ref, *refs):
    expands, contracts, out_ref = refs[:count], refs[count:-1], refs[-1]
    total = None
    for expand_ref, contract_ref in zip(expands, contracts):
        extent = expand_ref.shape[1]
        stride = math.gcd(extent, 512)
        for start in range(0, extent, stride):
            hidden = jnp.dot(
                rows_ref[...], expand_ref[:, start : start + stride], preferred_element_type=jnp.float32
            )
            hidden = jax.nn.gelu(hidden, approximate=True).astype(jnp.bfloat16)
            part = jnp.dot(
                hidden, contract_ref[start : start + stride], preferred_element_type=jnp.float32
            )
            total = part if total is None else total + part
    out_ref[...] = total


def feed_forward(rows, expands, contracts):
    extent = sum(e.shape[1] for e in expands)
    return pl.pallas_call(
        functools.partial(feed_forward_kernel, len(expands)),
        in_specs=[pl.BlockSpec(memory_space=pltpu.VMEM)] * (1 + len(expands) + len(contracts)),
        out_specs=pl.BlockSpec(memory_space=pltpu.VMEM),
        out_shape=jax.ShapeDtypeStruct(rows.shape, jnp.float32),
        cost_estimate=pl.CostEstimate(
            flops=4 * rows.size * extent, bytes_accessed=6 * rows.size, transcendentals=rows.shape[0] * extent
        ),
        compiler_params=pltpu.CompilerParams(vmem_limit_bytes=16 * 1024 * 1024),
    )(rows, *expands, *contracts)


def choose_prefix(own, owners, sizes):
    groups, members = sizes
    group_index = lax.axis_index("group")
    member_index = lax.axis_index("member")
    wanted = pick_value(owners, group_index)
    if groups != 4:
        every_block = lax.all_gather(own, "group", axis=0)
        return lax.dynamic_index_in_dim(every_block, wanted, 0, keepdims=False)
    near = 1 + member_index % 2
    far = 3 - near

    def step(block, flip):
        pairs = [
            (g * members + m, (g ^ (flip ^ (3 * (m % 2)))) * members + m)
            for g in range(groups)
            for m in range(members)
        ]
        return lax.ppermute(block, ("group", "member"), pairs)

    beside = step(own, 1)
    wanted_there = pick_value(owners, group_index ^ far)
    passed = jnp.where(wanted_there == (group_index ^ near), beside, own)
    across = step(passed, 2)
    return jnp.where(
        wanted == group_index, own, jnp.where(wanted == (group_index ^ near), beside, across)
    )


def shards(
    sizes,
    activations,
    lengths,
    assignment,
    owners,
    prefix_cache,
    first_gain,
    first_bias,
    query_weight,
    keyval_weight,
    output_weight,
    second_gain,
    second_bias,
    expand_weight,
    contract_weight,
):
    groups, members = sizes
    chips = members // 2
    order = ring_order(chips)
    after = {order[i]: order[(i + 1) % chips] for i in range(chips)}
    ring_pairs = [(2 * z + c, 2 * after[z] + c) for z in range(chips) for c in range(2)]
    swap_pairs = [(m, m ^ 1) for m in range(members)]
    ring = lambda block: lax.ppermute(block, "member", ring_pairs)
    swap = lambda block: lax.ppermute(block, "member", swap_pairs)

    member_index = lax.axis_index("member")
    request = pick_value(assignment[0], member_index)
    length_here = pick_value(lengths[0], request)
    tokens = activations[0]
    row_count = tokens.shape[0]
    head_size = prefix_cache.shape[2] // 2

    block = choose_prefix(prefix_cache[0], owners, sizes)
    expand_other = swap(expand_weight)
    contract_other = swap(contract_weight)

    tokens_wide = tokens.astype(jnp.float32)
    normed = layer_norm(tokens_wide, first_gain, first_bias).astype(jnp.bfloat16)
    factor = math.log2(math.e) / math.sqrt(head_size)
    queries = jnp.dot(normed, query_weight, preferred_element_type=jnp.float32)
    queries = (queries * factor).astype(jnp.bfloat16)
    keys_values = jnp.dot(normed, keyval_weight, preferred_element_type=jnp.float32).astype(
        jnp.bfloat16
    )

    expand_here, contract_here = hold(expand_weight, contract_weight)
    block, queries, keys_values, expand_other, contract_other = lax.optimization_barrier(
        (block, queries, keys_values, expand_other, contract_other)
    )

    state = None
    for step in range(chips):
        last = step == chips - 1
        later = None if last else ring(block)
        other = swap(block)
        state = attend(queries, keys_values, state, [block], False, head_size)
        state = attend(queries, keys_values, state, [other], last, head_size)
        if step == 0:
            expand_other, contract_other = hold(expand_other, contract_other)
        if not last:
            later, state = lax.optimization_barrier((later, state))
        block = later
    attended = state

    expands, contracts = (expand_here, expand_other), (contract_here, contract_other)
    residual = tokens_wide + jnp.dot(attended, output_weight, preferred_element_type=jnp.float32)
    second = layer_norm(residual, second_gain, second_bias).astype(jnp.bfloat16)

    rows, summed = second, None
    for step in range(1, chips):
        rows = ring(rows)
        if step == 1:
            here = feed_forward(second, expands, contracts)
        part = feed_forward(rows, expands, contracts)
        part = part if summed is None else part + summed.astype(jnp.float32)
        summed = ring(part.astype(jnp.bfloat16))
    total = residual + here + summed.astype(jnp.float32)
    is_live = lax.broadcasted_iota(jnp.int32, (row_count, 1), 0) < length_here
    return jnp.where(is_live, total, 0.0).astype(jnp.bfloat16)[None]


def solution(mesh):
    sizes = (mesh.shape["group"], mesh.shape["member"])
    return jax.shard_map(
        functools.partial(shards, sizes),
        mesh=mesh,
        in_specs=(
            P("group", "member", None),
            P("group", None),
            P("group", None),
            P(),
            P("group", "member", None),
            P(),
            P(),
            P(),
            P(),
            P(),
            P(),
            P(),
            P(None, "member"),
            P("member", None),
        ),
        out_specs=P("group", "member", None),
        check_vma=False,
    )
```

```python
import functools
import math

import jax
import jax.numpy as jnp
from jax import lax
from jax.experimental import pallas as pl
from jax.experimental.pallas import tpu as pltpu
from jax.sharding import PartitionSpec as P

EPSILON = 1e-05
NEGATIVE = -1e30
HEADS_AT_ONCE = 8
HEADS_STACKED = 2
PARTS = 2


def layer_norm(values, gain, bias):
    average = jnp.mean(values, axis=-1, keepdims=True)
    centered = values - average
    spread = jnp.mean(centered * centered, axis=-1, keepdims=True)
    return centered * lax.rsqrt(spread + EPSILON) * gain + bias


def pick_value(table, wanted):
    slots_at = lax.broadcasted_iota(jnp.int32, table.shape, 0)
    return jnp.sum(jnp.where(slots_at == wanted, table, 0))


def ring_order(chips):
    return list(range(0, 1)) + list(range(1, chips, 2)) + list(range(chips - 2 + chips % 2, 0, -2))


def attend_kernel(first, last, head_size, group, carried, *refs):
    refs = list(refs)
    if carried:
        semaphores = refs.pop()
        targets, refs = refs[-carried:], refs[:-carried]
        outs = 1 if last else 3
        sources = refs[-outs - carried : -outs]
        del refs[-outs - carried : -outs]
        copies = [
            pltpu.make_async_copy(source, target, semaphores.at[i])
            for i, (source, target) in enumerate(zip(sources, targets))
        ]

        @pl.when(pl.program_id(0) == 0)
        def _():
            for copy in copies:
                copy.start()

    query_ref = refs.pop(0)
    if first:
        own_ref = refs.pop(0)
    else:
        weighted_in, highest_in, denominator_in = refs[:3]
        del refs[:3]
    outs = 1 if last else 3
    block_refs, out_refs = refs[:-outs], refs[-outs:]
    rows = query_ref.shape[0]
    heads = query_ref.shape[1] // head_size
    parts = [jnp.concatenate([ref[...] for ref in block_refs], axis=0)]
    if first:
        parts.insert(0, own_ref[...])

    def stacked(ref, start):
        return jnp.concatenate(
            [ref[:, (start + h) * head_size : (start + h + 1) * head_size] for h in range(group)], axis=0
        )

    def all_scores(start):
        queries = stacked(query_ref, start)
        result = []
        for part in parts:
            scores = lax.dot_general(
                queries, part[:, :head_size], (((1,), (1,)), ((), ())), preferred_element_type=jnp.float32
            )
            result.append(scores)
        if first:
            row_at = lax.broadcasted_iota(jnp.int32, result[0].shape, 0) % rows
            column_at = lax.broadcasted_iota(jnp.int32, result[0].shape, 1)
            result[0] = jnp.where(column_at <= row_at, result[0], NEGATIVE)
        return result

    def fold(start, scores):
        highest = None
        for part in scores:
            top = jnp.max(part, axis=-1, keepdims=True)
            highest = top if highest is None else jnp.maximum(highest, top)
        weighted, denominator = None, None
        if not first:
            before = jnp.concatenate([highest_in[start + h] for h in range(group)], axis=0)
            highest = jnp.maximum(highest, before)
            rescale = jnp.exp2(before - highest)
            weighted = stacked(weighted_in, start) * rescale
            denominator = (
                jnp.concatenate([denominator_in[start + h] for h in range(group)], axis=0) * rescale
            )
        for part, ref in zip(scores, parts):
            exponent = jnp.exp2(part - highest)
            total = jnp.sum(exponent, axis=-1, keepdims=True)
            product = jnp.dot(
                exponent.astype(jnp.bfloat16), ref[:, head_size:], preferred_element_type=jnp.float32
            )
            weighted = product if weighted is None else weighted + product
            denominator = total if denominator is None else denominator + total
        if last:
            weighted = weighted / denominator
        for h in range(group):
            at = start + h
            part = slice(h * rows, (h + 1) * rows)
            out_refs[0][:, at * head_size : (at + 1) * head_size] = weighted[part].astype(out_refs[0].dtype)
            if not last:
                out_refs[1][at] = highest[part]
                out_refs[2][at] = denominator[part]

    scores = all_scores(0)
    for start in range(0, heads, group):
        following = all_scores(start + group) if start + group < heads else None
        fold(start, scores)
        scores = following

    if carried:

        @pl.when(pl.program_id(0) == pl.num_programs(0) - 1)
        def _():
            for copy in copies:
                copy.wait()


def attend(queries, own, state, blocks, last, head_size, share=(0, 1), carried=()):
    rows, width = queries.shape[0] // share[1], queries.shape[1]
    heads = width // head_size
    at_once = math.gcd(heads, HEADS_AT_ONCE * share[1])
    wide = at_once * head_size
    first = state is None
    flat = pl.BlockSpec((rows, wide), lambda i: (share[0], i))
    stat = pl.BlockSpec((at_once, rows, 1), lambda i: (i, share[0], 0))
    whole = lambda array: pl.BlockSpec(array.shape, lambda i: (0, 0))
    in_specs = [flat] + ([whole(own)] if first else [flat, stat, stat]) + [whole(b) for b in blocks]
    operands = [queries] + ([own] if first else list(state)) + list(blocks)
    if last:
        out_specs = [pl.BlockSpec((rows, wide), lambda i: (0, i))]
        out_shape = [jax.ShapeDtypeStruct((rows, width), jnp.bfloat16)]
    else:
        out_specs = [flat, stat, stat]
        out_shape = [jax.ShapeDtypeStruct((rows, width), jnp.float32)] + [
            jax.ShapeDtypeStruct((heads, rows, 1), jnp.float32)
        ] * 2
    keys = sum(b.shape[0] for b in blocks) + (own.shape[0] if first else 0)
    outs = len(out_shape)
    result = pl.pallas_call(
        functools.partial(
            attend_kernel, first, last, head_size, math.gcd(at_once, HEADS_STACKED * share[1]), len(carried)
        ),
        grid=(heads // at_once,),
        in_specs=in_specs + [pl.BlockSpec(memory_space=pltpu.HBM)] * len(carried),
        out_specs=out_specs + [pl.BlockSpec(memory_space=pl.ANY)] * len(carried),
        out_shape=out_shape + [pltpu.VMEM(w.shape, w.dtype) for w in carried],
        scratch_shapes=[pltpu.SemaphoreType.DMA((len(carried),))] if carried else [],
        cost_estimate=pl.CostEstimate(
            flops=0 if last else 4 * rows * width * keys,
            bytes_accessed=0 if last else 2 * keys * 2 * head_size + 8 * rows * width,
            transcendentals=0 if last else rows * heads * keys,
        ),
        compiler_params=pltpu.CompilerParams(vmem_limit_bytes=20 * 1024 * 1024),
    )(*operands, *carried)
    return (result[0] if last else list(result[:outs])), list(result[outs:])


def hold_kernel(count, *refs):
    sources, held, done_ref, semaphores = refs[:count], refs[count:-2], refs[-2], refs[-1]
    copies = [
        pltpu.make_async_copy(sources[i], held[i], semaphores.at[i]) for i in range(count)
    ]
    for copy in copies:
        copy.start()
    done_ref[...] = jnp.zeros_like(done_ref)
    for copy in copies:
        copy.wait()


def hold(weights, room):
    count = len(weights)
    size = sum(w.size * w.dtype.itemsize for w in weights)
    return pl.pallas_call(
        functools.partial(hold_kernel, count),
        in_specs=[pl.BlockSpec(memory_space=pltpu.HBM)] * count,
        out_specs=[pl.BlockSpec(memory_space=pltpu.VMEM)] * (count + 1),
        out_shape=[pltpu.VMEM(w.shape, w.dtype) for w in weights] + [jax.ShapeDtypeStruct((8, 128), jnp.float32)],
        scratch_shapes=[pltpu.SemaphoreType.DMA((count,))],
        cost_estimate=pl.CostEstimate(flops=0, bytes_accessed=size, transcendentals=0),
        compiler_params=pltpu.CompilerParams(vmem_limit_bytes=room * 1024 * 1024),
    )(*weights)


def feed_forward_kernel(count, rows_ref, *refs):
    expands, contracts, out_ref = refs[:count], refs[count : 2 * count], refs[-1]
    out_ref[...] = jnp.zeros_like(out_ref)
    for expand_ref, contract_ref in zip(expands, contracts):
        extent = expand_ref.shape[1]
        stride = math.gcd(extent, 512)

        @pl.loop(0, extent // stride)
        def _(index):
            at = pl.ds(pl.multiple_of(index * stride, stride), stride)
            hidden = jnp.dot(rows_ref[...], expand_ref[:, at], preferred_element_type=jnp.float32)
            hidden = jax.nn.gelu(hidden, approximate=True).astype(jnp.bfloat16)
            out_ref[...] += jnp.dot(hidden, contract_ref[at, :], preferred_element_type=jnp.float32)


def feed_forward(rows, expands, contracts, held):
    return pl.pallas_call(
        functools.partial(feed_forward_kernel, len(expands)),
        in_specs=[pl.BlockSpec(memory_space=pltpu.VMEM)] * (1 + len(expands) + len(contracts) + len(held)),
        out_specs=pl.BlockSpec(memory_space=pltpu.VMEM),
        out_shape=jax.ShapeDtypeStruct(rows.shape, jnp.float32),
        cost_estimate=pl.CostEstimate(flops=0, bytes_accessed=0, transcendentals=0),
        compiler_params=pltpu.CompilerParams(vmem_limit_bytes=16 * 1024 * 1024),
    )(rows, *expands, *contracts, *held)


def finish_kernel(share, attended_ref, weight_ref, tokens_ref, gain_ref, bias_ref, residual_ref, second_ref):
    rows = attended_ref.shape[0]
    tokens = tokens_ref[share * rows : (share + 1) * rows].astype(jnp.float32)
    residual = tokens + jnp.dot(
        attended_ref[...], weight_ref[...], preferred_element_type=jnp.float32
    )
    residual_ref[...] = residual
    second_ref[...] = layer_norm(residual, gain_ref[...], bias_ref[...]).astype(jnp.bfloat16)


def finish(attended, weight, tokens, gain, bias, share):
    inside = pl.BlockSpec(memory_space=pltpu.VMEM)
    return pl.pallas_call(
        functools.partial(finish_kernel, share),
        in_specs=[inside] * 5,
        out_specs=[inside] * 2,
        out_shape=[
            jax.ShapeDtypeStruct(attended.shape, jnp.float32),
            jax.ShapeDtypeStruct(attended.shape, jnp.bfloat16),
        ],
        cost_estimate=pl.CostEstimate(flops=0, bytes_accessed=0, transcendentals=0),
        compiler_params=pltpu.CompilerParams(vmem_limit_bytes=16 * 1024 * 1024),
    )(attended, weight, tokens, gain[None], bias[None])


def first_hop(own, owners, sizes):
    groups, members = sizes
    group_index = lax.axis_index("group")
    member_index = lax.axis_index("member")
    wanted = pick_value(owners, group_index)
    if groups != 4:
        every_block = lax.all_gather(own, "group", axis=0)
        chosen = lax.dynamic_index_in_dim(every_block, wanted, 0, keepdims=False)
        return chosen, lambda chosen: chosen
    near = 1 + member_index % 2
    far = 3 - near

    def step(block, flip):
        pairs = [
            (g * members + m, (g ^ (flip ^ (3 * (m % 2)))) * members + m)
            for g in range(groups)
            for m in range(members)
        ]
        return lax.ppermute(block, ("group", "member"), pairs)

    wanted_there = pick_value(owners, group_index ^ far)

    def second_hop(beside):
        passed = jnp.where(wanted_there == (group_index ^ near), beside, own)
        across = step(passed, 2)
        return jnp.where(
            wanted == group_index, own, jnp.where(wanted == (group_index ^ near), beside, across)
        )

    return step(own, 1), second_hop


def project_kernel(
    factor, tokens_ref, gain_ref, bias_ref, query_ref, keyval_ref, queries_ref, keys_values_ref, held, semaphores
):
    count, _, stride = held.shape
    copies = [
        pltpu.make_async_copy(
            query_ref.at[:, pl.ds(i * stride, stride)], held.at[i], semaphores.at[i]
        )
        for i in range(count)
    ]
    for copy in copies:
        copy.start()
    values = tokens_ref[...].astype(jnp.float32)
    normed = layer_norm(values, gain_ref[...], bias_ref[...]).astype(jnp.bfloat16)
    keys_values_ref[...] = jnp.dot(
        normed, keyval_ref[...], preferred_element_type=jnp.float32
    ).astype(jnp.bfloat16)
    for i, copy in enumerate(copies):
        copy.wait()
        queries = jnp.dot(normed, held[i], preferred_element_type=jnp.float32)
        queries_ref[:, i * stride : (i + 1) * stride] = (queries * factor).astype(jnp.bfloat16)


def project(tokens, gain, bias, query_weight, keyval_weight, factor):
    rows, width = tokens.shape
    wide, narrow = query_weight.shape[1], keyval_weight.shape[1]
    stride = math.gcd(wide, 512)
    inside = pl.BlockSpec(memory_space=pltpu.VMEM)
    return pl.pallas_call(
        functools.partial(project_kernel, factor),
        in_specs=[inside, inside, inside, pl.BlockSpec(memory_space=pltpu.HBM), inside],
        out_specs=[inside, inside],
        out_shape=[
            jax.ShapeDtypeStruct((rows, wide), jnp.bfloat16),
            jax.ShapeDtypeStruct((rows, narrow), jnp.bfloat16),
        ],
        scratch_shapes=[
            pltpu.VMEM((wide // stride, width, stride), jnp.bfloat16),
            pltpu.SemaphoreType.DMA((wide // stride,)),
        ],
        cost_estimate=pl.CostEstimate(
            flops=2 * rows * width * (wide + narrow),
            bytes_accessed=2 * width * (wide + narrow),
            transcendentals=rows,
        ),
        compiler_params=pltpu.CompilerParams(vmem_limit_bytes=58 * 1024 * 1024),
    )(tokens, gain[None], bias[None], query_weight, keyval_weight)


def shards(
    sizes,
    activations,
    lengths,
    assignment,
    owners,
    prefix_cache,
    first_gain,
    first_bias,
    query_weight,
    keyval_weight,
    output_weight,
    second_gain,
    second_bias,
    expand_weight,
    contract_weight,
):
    groups, members = sizes
    chips = members // 2
    order = ring_order(chips)
    after = {order[i]: order[(i + 1) % chips] for i in range(chips)}
    ring_pairs = [(2 * z + c, 2 * after[z] + c) for z in range(chips) for c in range(2)]
    swap_pairs = [(m, m ^ 1) for m in range(members)]
    ring = lambda block: lax.ppermute(block, "member", ring_pairs)
    swap = lambda block: lax.ppermute(block, "member", swap_pairs)

    tokens = activations[0]
    row_count = tokens.shape[0]
    head_size = prefix_cache.shape[2] // 2

    beside, second_hop = first_hop(prefix_cache[0], owners, sizes)
    expand_other = swap(expand_weight)
    contract_other = swap(contract_weight)

    factor = math.log2(math.e) / math.sqrt(head_size)
    queries, keys_values = project(
        tokens, first_gain, first_bias, query_weight, keyval_weight, factor
    )
    beside, queries, keys_values, expand_other = lax.optimization_barrier(
        (beside, queries, keys_values, expand_other)
    )
    block = second_hop(beside)
    expand_here, contract_here, held_here = hold((expand_weight, contract_weight), 50)
    block, held_here, contract_other = lax.optimization_barrier((block, held_here, contract_other))

    count = chips * PARTS
    pieces = list(jnp.split(block, PARTS))
    pieces += [ring(piece) for piece in pieces] if chips > 1 else []
    work = [pieces[:PARTS], [swap(block)]]
    state, carried, held = None, [expand_other, contract_other], []
    for i in range(PARTS, count):
        state, brought = attend(
            queries, keys_values, state, work.pop(0), False, head_size, carried=carried[:1]
        )
        carried, held = carried[1:], held + brought
        pieces[i], state = lax.optimization_barrier((pieces[i], state))
        if i + PARTS < count:
            pieces.append(ring(pieces[i]))
        work.append([pieces[i], swap(pieces[i])])
    while len(work) > 1:
        state, brought = attend(
            queries, keys_values, state, work.pop(0), False, head_size, carried=carried[:1]
        )
        carried, held = carried[1:], held + brought
    expand_other, contract_other = held

    blocks, residual, rows = work[0], [], []
    for i in range(PARTS):
        attended, _ = attend(queries, keys_values, state, blocks, True, head_size, (i, PARTS))
        ahead, behind = finish(attended, output_weight, tokens, second_gain, second_bias, i)
        residual.append(ahead)
        rows.append(behind)
        blocks[0], rows[i] = lax.optimization_barrier((blocks[0], rows[i]))

    expands, contracts = (expand_here, expand_other), (contract_here, contract_other)
    held = [held_here]
    second = jnp.concatenate(rows, axis=0)
    arriving = [ring(part) for part in rows]
    before, summed = None, [None] * PARTS
    for step in range(1, chips):
        for i in range(PARTS):
            if before is None:
                rows[i] = arriving[i]
            else:
                rows[i], before = lax.optimization_barrier((arriving[i], before))
            if step < chips - 1:
                arriving[i] = ring(rows[i])
            part = feed_forward(rows[i], expands, contracts, held)
            before = part
            part = part if step == 1 else part + summed[i].astype(jnp.float32)
            summed[i] = ring(part.astype(jnp.bfloat16))
    second, before, lengths, assignment = lax.optimization_barrier(
        (second, before, lengths, assignment)
    )
    here = feed_forward(second, expands, contracts, held)
    total = jnp.concatenate(residual, axis=0) + here + jnp.concatenate(summed, axis=0).astype(jnp.float32)
    member_index = lax.axis_index("member")
    request = pick_value(assignment[0], member_index)
    length_here = pick_value(lengths[0], request)
    is_live = lax.broadcasted_iota(jnp.int32, (row_count, 1), 0) < length_here
    return jnp.where(is_live, total, 0.0).astype(jnp.bfloat16)[None]


def solution(mesh):
    sizes = (mesh.shape["group"], mesh.shape["member"])
    return jax.shard_map(
        functools.partial(shards, sizes),
        mesh=mesh,
        in_specs=(
            P("group", "member", None),
            P("group", None),
            P("group", None),
            P(),
            P("group", "member", None),
            P(),
            P(),
            P(),
            P(),
            P(),
            P(),
            P(),
            P(None, "member"),
            P("member", None),
        ),
        out_specs=P("group", "member", None),
        check_vma=False,
    )
```

```python
import functools
import math

import jax
import jax.numpy as jnp
from jax import lax
from jax.experimental import pallas as pl
from jax.experimental.pallas import tpu as pltpu
from jax.sharding import PartitionSpec as P

EPSILON = 1e-05
NEGATIVE = -1e30
HEADS_AT_ONCE = 8
HEADS_STACKED = 2
PARTS = 2


def layer_norm(values, gain, bias):
    average = jnp.mean(values, axis=-1, keepdims=True)
    centered = values - average
    spread = jnp.mean(centered * centered, axis=-1, keepdims=True)
    return centered * lax.rsqrt(spread + EPSILON) * gain + bias


def pick_value(table, wanted):
    slots_at = lax.broadcasted_iota(jnp.int32, table.shape, 0)
    return jnp.sum(jnp.where(slots_at == wanted, table, 0))


def ring_order(chips):
    return list(range(0, 1)) + list(range(1, chips, 2)) + list(range(chips - 2 + chips % 2, 0, -2))


def attend_kernel(first, last, head_size, group, carried, *refs):
    refs = list(refs)
    if carried:
        semaphores = refs.pop()
        targets, refs = refs[-carried:], refs[:-carried]
        outs = 1 if last else 3
        sources = refs[-outs - carried : -outs]
        del refs[-outs - carried : -outs]
        copies = [
            pltpu.make_async_copy(source, target, semaphores.at[i])
            for i, (source, target) in enumerate(zip(sources, targets))
        ]

        @pl.when(pl.program_id(0) == 0)
        def _():
            for copy in copies:
                copy.start()

    query_ref = refs.pop(0)
    if first:
        own_ref = refs.pop(0)
    else:
        weighted_in, highest_in, denominator_in = refs[:3]
        del refs[:3]
    outs = 1 if last else 3
    block_refs, out_refs = refs[:-outs], refs[-outs:]
    rows = query_ref.shape[0]
    heads = query_ref.shape[1] // head_size
    parts = [jnp.concatenate([ref[...] for ref in block_refs], axis=0)]
    if first:
        parts.insert(0, own_ref[...])
    summing = [
        jnp.concatenate([part[:, head_size:], jnp.ones_like(part[:, head_size:])], axis=1) for part in parts
    ]

    def stacked(ref, start):
        return jnp.concatenate(
            [ref[:, (start + h) * head_size : (start + h + 1) * head_size] for h in range(group)], axis=0
        )

    def all_scores(start):
        queries = stacked(query_ref, start)
        result = []
        for part in parts:
            scores = lax.dot_general(
                queries, part[:, :head_size], (((1,), (1,)), ((), ())), preferred_element_type=jnp.float32
            )
            result.append(scores)
        if first:
            row_at = lax.broadcasted_iota(jnp.int32, result[0].shape, 0) % rows
            column_at = lax.broadcasted_iota(jnp.int32, result[0].shape, 1)
            result[0] = jnp.where(column_at <= row_at, result[0], NEGATIVE)
        return result

    def fold(start, scores):
        highest = None
        for part in scores:
            top = jnp.max(part, axis=-1, keepdims=True)
            highest = top if highest is None else jnp.maximum(highest, top)
        weighted, denominator = None, None
        if not first:
            before = jnp.concatenate([highest_in[start + h] for h in range(group)], axis=0)
            highest = jnp.maximum(highest, before)
            rescale = jnp.exp2(before - highest)
            weighted = stacked(weighted_in, start) * rescale
            denominator = (
                jnp.concatenate([denominator_in[start + h] for h in range(group)], axis=0) * rescale
            )
        for part, keyed in zip(scores, summing):
            exponent = jnp.exp2(part - highest)
            product = jnp.dot(
                exponent.astype(jnp.bfloat16), keyed, preferred_element_type=jnp.float32
            )
            product, total = product[:, :head_size], product[:, head_size : head_size + 1]
            weighted = product if weighted is None else weighted + product
            denominator = total if denominator is None else denominator + total
        if last:
            weighted = weighted / denominator
        for h in range(group):
            at = start + h
            part = slice(h * rows, (h + 1) * rows)
            out_refs[0][:, at * head_size : (at + 1) * head_size] = weighted[part].astype(out_refs[0].dtype)
            if not last:
                out_refs[1][at] = highest[part]
                out_refs[2][at] = denominator[part]

    scores = all_scores(0)
    for start in range(0, heads, group):
        following = all_scores(start + group) if start + group < heads else None
        fold(start, scores)
        scores = following

    if carried:

        @pl.when(pl.program_id(0) == pl.num_programs(0) - 1)
        def _():
            for copy in copies:
                copy.wait()


def attend(queries, own, state, blocks, last, head_size, share=(0, 1), carried=()):
    rows, width = queries.shape[0] // share[1], queries.shape[1]
    heads = width // head_size
    at_once = math.gcd(heads, HEADS_AT_ONCE * share[1])
    wide = at_once * head_size
    first = state is None
    flat = pl.BlockSpec((rows, wide), lambda i: (share[0], i))
    stat = pl.BlockSpec((at_once, rows, 1), lambda i: (i, share[0], 0))
    whole = lambda array: pl.BlockSpec(array.shape, lambda i: (0, 0))
    in_specs = [flat] + ([whole(own)] if first else [flat, stat, stat]) + [whole(b) for b in blocks]
    operands = [queries] + ([own] if first else list(state)) + list(blocks)
    if last:
        out_specs = [pl.BlockSpec((rows, wide), lambda i: (0, i))]
        out_shape = [jax.ShapeDtypeStruct((rows, width), jnp.bfloat16)]
    else:
        out_specs = [flat, stat, stat]
        out_shape = [jax.ShapeDtypeStruct((rows, width), jnp.float32)] + [
            jax.ShapeDtypeStruct((heads, rows, 1), jnp.float32)
        ] * 2
    keys = sum(b.shape[0] for b in blocks) + (own.shape[0] if first else 0)
    outs = len(out_shape)
    result = pl.pallas_call(
        functools.partial(
            attend_kernel, first, last, head_size, math.gcd(at_once, HEADS_STACKED * share[1]), len(carried)
        ),
        grid=(heads // at_once,),
        in_specs=in_specs + [pl.BlockSpec(memory_space=pltpu.HBM)] * len(carried),
        out_specs=out_specs + [pl.BlockSpec(memory_space=pl.ANY)] * len(carried),
        out_shape=out_shape + [pltpu.VMEM(w.shape, w.dtype) for w in carried],
        scratch_shapes=[pltpu.SemaphoreType.DMA((len(carried),))] if carried else [],
        cost_estimate=pl.CostEstimate(
            flops=0 if last else 4 * rows * width * keys,
            bytes_accessed=0 if last else 2 * keys * 2 * head_size + 8 * rows * width,
            transcendentals=0 if last else rows * heads * keys,
        ),
        compiler_params=pltpu.CompilerParams(vmem_limit_bytes=20 * 1024 * 1024),
    )(*operands, *carried)
    return (result[0] if last else list(result[:outs])), list(result[outs:])


def hold_kernel(count, *refs):
    sources, held, done_ref, semaphores = refs[:count], refs[count:-2], refs[-2], refs[-1]
    copies = [
        pltpu.make_async_copy(sources[i], held[i], semaphores.at[i]) for i in range(count)
    ]
    for copy in copies:
        copy.start()
    done_ref[...] = jnp.zeros_like(done_ref)
    for copy in copies:
        copy.wait()


def hold(weights, room):
    count = len(weights)
    size = sum(w.size * w.dtype.itemsize for w in weights)
    return pl.pallas_call(
        functools.partial(hold_kernel, count),
        in_specs=[pl.BlockSpec(memory_space=pltpu.HBM)] * count,
        out_specs=[pl.BlockSpec(memory_space=pltpu.VMEM)] * (count + 1),
        out_shape=[pltpu.VMEM(w.shape, w.dtype) for w in weights] + [jax.ShapeDtypeStruct((8, 128), jnp.float32)],
        scratch_shapes=[pltpu.SemaphoreType.DMA((count,))],
        cost_estimate=pl.CostEstimate(flops=0, bytes_accessed=size, transcendentals=0),
        compiler_params=pltpu.CompilerParams(vmem_limit_bytes=room * 1024 * 1024),
    )(*weights)


def feed_forward_kernel(count, rows_ref, *refs):
    expands, contracts, out_ref = refs[:count], refs[count : 2 * count], refs[-1]
    out_ref[...] = jnp.zeros_like(out_ref)
    for expand_ref, contract_ref in zip(expands, contracts):
        extent = expand_ref.shape[1]
        stride = math.gcd(extent, 512)

        @pl.loop(0, extent // stride)
        def _(index):
            at = pl.ds(pl.multiple_of(index * stride, stride), stride)
            hidden = jnp.dot(rows_ref[...], expand_ref[:, at], preferred_element_type=jnp.float32)
            hidden = jax.nn.gelu(hidden, approximate=True).astype(jnp.bfloat16)
            out_ref[...] += jnp.dot(hidden, contract_ref[at, :], preferred_element_type=jnp.float32)


def feed_forward(rows, expands, contracts, held):
    return pl.pallas_call(
        functools.partial(feed_forward_kernel, len(expands)),
        in_specs=[pl.BlockSpec(memory_space=pltpu.VMEM)] * (1 + len(expands) + len(contracts) + len(held)),
        out_specs=pl.BlockSpec(memory_space=pltpu.VMEM),
        out_shape=jax.ShapeDtypeStruct(rows.shape, jnp.float32),
        cost_estimate=pl.CostEstimate(flops=0, bytes_accessed=0, transcendentals=0),
        compiler_params=pltpu.CompilerParams(vmem_limit_bytes=16 * 1024 * 1024),
    )(rows, *expands, *contracts, *held)


def finish_kernel(share, attended_ref, weight_ref, tokens_ref, gain_ref, bias_ref, residual_ref, second_ref):
    rows = attended_ref.shape[0]
    tokens = tokens_ref[share * rows : (share + 1) * rows].astype(jnp.float32)
    residual = tokens + jnp.dot(
        attended_ref[...], weight_ref[...], preferred_element_type=jnp.float32
    )
    residual_ref[...] = residual
    second_ref[...] = layer_norm(residual, gain_ref[...], bias_ref[...]).astype(jnp.bfloat16)


def finish(attended, weight, tokens, gain, bias, share):
    inside = pl.BlockSpec(memory_space=pltpu.VMEM)
    return pl.pallas_call(
        functools.partial(finish_kernel, share),
        in_specs=[inside] * 5,
        out_specs=[inside] * 2,
        out_shape=[
            jax.ShapeDtypeStruct(attended.shape, jnp.float32),
            jax.ShapeDtypeStruct(attended.shape, jnp.bfloat16),
        ],
        cost_estimate=pl.CostEstimate(flops=0, bytes_accessed=0, transcendentals=0),
        compiler_params=pltpu.CompilerParams(vmem_limit_bytes=16 * 1024 * 1024),
    )(attended, weight, tokens, gain[None], bias[None])


def first_hop(own, owners, sizes):
    groups, members = sizes
    group_index = lax.axis_index("group")
    member_index = lax.axis_index("member")
    wanted = pick_value(owners, group_index)
    if groups != 4:
        every_block = lax.all_gather(own, "group", axis=0)
        chosen = lax.dynamic_index_in_dim(every_block, wanted, 0, keepdims=False)
        return chosen, lambda chosen: chosen
    near = 1 + member_index % 2
    far = 3 - near

    def step(block, flip):
        pairs = [
            (g * members + m, (g ^ (flip ^ (3 * (m % 2)))) * members + m)
            for g in range(groups)
            for m in range(members)
        ]
        return lax.ppermute(block, ("group", "member"), pairs)

    wanted_there = pick_value(owners, group_index ^ far)

    def second_hop(beside):
        passed = jnp.where(wanted_there == (group_index ^ near), beside, own)
        across = step(passed, 2)
        return jnp.where(
            wanted == group_index, own, jnp.where(wanted == (group_index ^ near), beside, across)
        )

    return step(own, 1), second_hop


def project_kernel(
    factor, tokens_ref, gain_ref, bias_ref, query_ref, keyval_ref, queries_ref, keys_values_ref, held, semaphores
):
    count, _, stride = held.shape
    copies = [
        pltpu.make_async_copy(
            query_ref.at[:, pl.ds(i * stride, stride)], held.at[i], semaphores.at[i]
        )
        for i in range(count)
    ]
    for copy in copies:
        copy.start()
    values = tokens_ref[...].astype(jnp.float32)
    normed = layer_norm(values, gain_ref[...], bias_ref[...]).astype(jnp.bfloat16)
    keys_values_ref[...] = jnp.dot(
        normed, keyval_ref[...], preferred_element_type=jnp.float32
    ).astype(jnp.bfloat16)
    for i, copy in enumerate(copies):
        copy.wait()
        queries = jnp.dot(normed, held[i], preferred_element_type=jnp.float32)
        queries_ref[:, i * stride : (i + 1) * stride] = (queries * factor).astype(jnp.bfloat16)


def project(tokens, gain, bias, query_weight, keyval_weight, factor):
    rows, width = tokens.shape
    wide, narrow = query_weight.shape[1], keyval_weight.shape[1]
    stride = math.gcd(wide, 512)
    inside = pl.BlockSpec(memory_space=pltpu.VMEM)
    return pl.pallas_call(
        functools.partial(project_kernel, factor),
        in_specs=[inside, inside, inside, pl.BlockSpec(memory_space=pltpu.HBM), inside],
        out_specs=[inside, inside],
        out_shape=[
            jax.ShapeDtypeStruct((rows, wide), jnp.bfloat16),
            jax.ShapeDtypeStruct((rows, narrow), jnp.bfloat16),
        ],
        scratch_shapes=[
            pltpu.VMEM((wide // stride, width, stride), jnp.bfloat16),
            pltpu.SemaphoreType.DMA((wide // stride,)),
        ],
        cost_estimate=pl.CostEstimate(
            flops=2 * rows * width * (wide + narrow),
            bytes_accessed=2 * width * (wide + narrow),
            transcendentals=rows,
        ),
        compiler_params=pltpu.CompilerParams(vmem_limit_bytes=58 * 1024 * 1024),
    )(tokens, gain[None], bias[None], query_weight, keyval_weight)


def shards(
    sizes,
    activations,
    lengths,
    assignment,
    owners,
    prefix_cache,
    first_gain,
    first_bias,
    query_weight,
    keyval_weight,
    output_weight,
    second_gain,
    second_bias,
    expand_weight,
    contract_weight,
):
    groups, members = sizes
    chips = members // 2
    order = ring_order(chips)
    after = {order[i]: order[(i + 1) % chips] for i in range(chips)}
    ring_pairs = [(2 * z + c, 2 * after[z] + c) for z in range(chips) for c in range(2)]
    swap_pairs = [(m, m ^ 1) for m in range(members)]
    ring = lambda block: lax.ppermute(block, "member", ring_pairs)
    swap = lambda block: lax.ppermute(block, "member", swap_pairs)

    tokens = activations[0]
    row_count = tokens.shape[0]
    head_size = prefix_cache.shape[2] // 2

    beside, second_hop = first_hop(prefix_cache[0], owners, sizes)
    expand_other = swap(expand_weight)
    contract_other = swap(contract_weight)

    factor = math.log2(math.e) / math.sqrt(head_size)
    queries, keys_values = project(
        tokens, first_gain, first_bias, query_weight, keyval_weight, factor
    )
    beside, queries, keys_values, expand_other = lax.optimization_barrier(
        (beside, queries, keys_values, expand_other)
    )
    block = second_hop(beside)
    expand_here, contract_here, held_here = hold((expand_weight, contract_weight), 50)
    block, held_here, contract_other = lax.optimization_barrier((block, held_here, contract_other))

    count = chips * PARTS
    pieces = list(jnp.split(block, PARTS))
    pieces += [ring(piece) for piece in pieces] if chips > 1 else []
    work = [pieces[:PARTS], [swap(block)]]
    state, carried, held = None, [expand_other, contract_other], []
    for i in range(PARTS, count):
        state, brought = attend(
            queries, keys_values, state, work.pop(0), False, head_size, carried=carried[:1]
        )
        carried, held = carried[1:], held + brought
        pieces[i], state = lax.optimization_barrier((pieces[i], state))
        if i + PARTS < count:
            pieces.append(ring(pieces[i]))
        work.append([pieces[i], swap(pieces[i])])
    while len(work) > 1:
        state, brought = attend(
            queries, keys_values, state, work.pop(0), False, head_size, carried=carried[:1]
        )
        carried, held = carried[1:], held + brought
    expand_other, contract_other = held

    blocks, residual, rows = work[0], [], []
    for i in range(PARTS):
        attended, _ = attend(queries, keys_values, state, blocks, True, head_size, (i, PARTS))
        ahead, behind = finish(attended, output_weight, tokens, second_gain, second_bias, i)
        residual.append(ahead)
        rows.append(behind)
        blocks[0], rows[i] = lax.optimization_barrier((blocks[0], rows[i]))

    expands, contracts = (expand_here, expand_other), (contract_here, contract_other)
    held = [held_here]
    second = jnp.concatenate(rows, axis=0)
    arriving = [ring(part) for part in rows]
    before, summed = None, [None] * PARTS
    for step in range(1, chips):
        for i in range(PARTS):
            if before is None:
                rows[i] = arriving[i]
            else:
                rows[i], before = lax.optimization_barrier((arriving[i], before))
            if step < chips - 1:
                arriving[i] = ring(rows[i])
            part = feed_forward(rows[i], expands, contracts, held)
            before = part
            part = part if step == 1 else part + summed[i].astype(jnp.float32)
            summed[i] = ring(part.astype(jnp.bfloat16))
    second, before, lengths, assignment = lax.optimization_barrier(
        (second, before, lengths, assignment)
    )
    here = feed_forward(second, expands, contracts, held)
    total = jnp.concatenate(residual, axis=0) + here + jnp.concatenate(summed, axis=0).astype(jnp.float32)
    member_index = lax.axis_index("member")
    request = pick_value(assignment[0], member_index)
    length_here = pick_value(lengths[0], request)
    is_live = lax.broadcasted_iota(jnp.int32, (row_count, 1), 0) < length_here
    return jnp.where(is_live, total, 0.0).astype(jnp.bfloat16)[None]


def solution(mesh):
    sizes = (mesh.shape["group"], mesh.shape["member"])
    return jax.shard_map(
        functools.partial(shards, sizes),
        mesh=mesh,
        in_specs=(
            P("group", "member", None),
            P("group", None),
            P("group", None),
            P(),
            P("group", "member", None),
            P(),
            P(),
            P(),
            P(),
            P(),
            P(),
            P(),
            P(None, "member"),
            P("member", None),
        ),
        out_specs=P("group", "member", None),
        check_vma=False,
    )
```
